32 devices in a mesh: ind: 4 (over y, x), var: 8 (over z, core).
Axes of the slice: x: 2, y: 2, z: 4, core: 2. Of those that a mesh axis runs over, the one named last changes fastest.
Arguments:
- genotypes: bfloat16 [1024, 393216], P('var', 'ind'), may hold values from -6 to 6, as said below
- residual: float32 [393216], P('ind'), may hold values from -6 to 6
- ancestry: int32 [393216], P('ind'), may hold values from 0 to 4, never falling along the last dimension, each value on 1 to 196608 neighbouring positions
- effects: float32 [5, 1024], P(None, 'var'), may hold values from -4 to 4
- prior_precision: float32 [5, 5], replicated, may hold values from -12 to 12, as said below
- noise_var: float32 [5], replicated, may hold values from 0.5 to 2
- block_index: int32 [3, 256], P(None, 'var'), may hold values from 0 to 127, as said below
- gaussians: float32 [3, 5, 256], P(None, None, 'var'), may hold values from -5 to 5
Outputs:
- new_residual: float32 [393216], P(('ind', 'var'))
- new_effects: float32 [5, 1024], P(None, 'var')
The draws below stay inside these ranges and needn't reach their ends.
Inputs may be any that keep to these rules, and one draw needn't show every extreme that they name: Scaled genotypes; variants and individuals have different scales. `prior_precision`: symmetric positive definite. `block_index`: in each step the 32 entries held by one index of var are distinct rows among that index's 128 variants; rows 0 and 127 appear in every draw.
All inputs are finite; a program needn't handle non-finite values.
Results may differ from the reference program's by a relative error of at most 0.0003.
Values sent between devices are 32-bit elements; how exact they have to be, the bound alone decides.
No kernel may reach another device: no remote copies, remote signals or barrier semaphores. Data moves between devices by JAX's collectives and lax.ppermute only.
A program may use at most 128 MiB of HBM per device.

```python
import math
import jax
import jax.numpy as jnp
import numpy as np
from jax import lax

K = 5
COLS = 128
BV = 32
STEPS = 3
NI = 393216
M = 1024
BLOCK = 256
N_VAR = 8


def draw_genotypes(key, part):
    col_key = jax.random.fold_in(key, 11)
    row_key = jax.random.fold_in(key, 12)
    base_key = jax.random.fold_in(key, 13)
    col_scale = jnp.exp(jax.random.uniform(col_key, (M, 1), jnp.float32, jnp.log(0.3), jnp.log(3.0)))
    row_scale = jnp.exp(jax.random.uniform(row_key, (1, NI), jnp.float32, jnp.log(0.3), jnp.log(3.0)))
    base = jnp.clip(jax.random.normal(base_key, (M, NI), jnp.float32), -4.0, 4.0)
    values = col_scale * row_scale * base / jnp.sqrt(jnp.float32(NI / K))
    return values.astype(jnp.bfloat16)


def draw_prior_precision(key, part):
    inner_key = jax.random.fold_in(key, 21)
    factor = 0.6 * jnp.clip(jax.random.normal(inner_key, (K, K), jnp.float32), -2.5, 2.5)
    return 0.5 * jnp.eye(K, dtype=jnp.float32) + jnp.dot(factor, factor.T)


def draw_block_index(key, part):
    groups = BLOCK // BV
    order_key = jax.random.fold_in(key, 31)
    column = jnp.arange(COLS, dtype=jnp.int32)
    ranking = jax.random.randint(order_key, (STEPS, groups, COLS), 0, 1 << 20, dtype=jnp.int32) * COLS + column
    first = (jnp.arange(STEPS)[:, None, None] == 0) & (jnp.arange(groups)[None, :, None] == 0)
    ends = (column == 0) | (column == COLS - 1)
    ranking = jnp.where(first & ends[None, None, :], -1 - column, ranking)
    order = jnp.argsort(ranking, axis=2, stable=True)[:, :, :BV]
    return order.reshape(STEPS, BLOCK).astype(jnp.int32)


def level_of(stream_key, extent, cuts, smallest, largest):
    level, own = 1.0, jax.random.fold_in(stream_key, 6)
    for axis_at, blocks in cuts:
        heights = jnp.exp(jax.random.uniform(jax.random.fold_in(own, axis_at), (blocks,), jnp.float32, smallest / len(cuts), largest / len(cuts)))
        level = level * jnp.repeat(heights, extent[axis_at] // blocks).reshape([-1 if axis == axis_at else 1 for axis in range(len(extent))])
    return level


def length_profile(number_of, total, limit, skew):
    weights = [(1 << 20) // math.isqrt(grade ** skew) + 1 for grade in range(2, number_of + 1)]
    rest, counts = total - limit - (number_of - 1), [1] * (number_of - 1)
    while rest > 0:
        candidates = [i for i in range(number_of - 1) if counts[i] < limit]
        mass, left = sum([weights[i] for i in candidates]), rest
        for i in candidates:
            addition = min(limit - counts[i], max(1, left * weights[i] // mass), rest)
            counts[i] = counts[i] + addition
            rest = rest - addition
    return np.array([limit] + counts)


def ragged(own_key, count, total, most, lean):
    if count == 2:
        one = jax.random.randint(own_key, (), max(1, total - most), min(most, total - 1) + 1)
        return jnp.stack([one, total - one])
    sizes = jnp.asarray(length_profile(count, total, most, lean), jnp.int32)
    pairs = (count - 1) // 2
    giver, sink = sizes[1:1 + 2 * pairs:2], sizes[2:2 + 2 * pairs:2]
    slack = jnp.minimum(giver - 1, most - sink)
    moved = jax.random.randint(jax.random.fold_in(own_key, 1), (pairs,), 0, 1 << 20) % (slack + 1)
    sizes = sizes.at[1:1 + 2 * pairs:2].set(giver - moved).at[2:2 + 2 * pairs:2].set(sink + moved)
    return sizes[jax.random.permutation(jax.random.fold_in(own_key, 2), count)]


def scatter_about(key, extent, scale, reach, cuts=(), kind=jnp.bfloat16):
    factor_of = level_of(key, extent, cuts, -0.22, 0.18) if cuts else 1.0
    result = jax.random.normal(key, extent, jnp.float32) * scale * factor_of
    return jnp.minimum(jnp.maximum(result, -reach), reach).astype(kind)


def setup_inputs(seed: int = 0) -> dict:
    key_list = jax.random.split(jax.random.key(seed), 9)
    genotypes = draw_genotypes(jax.random.fold_in(key_list[8], 71), 0)
    residual = scatter_about(key_list[1], (NI,), 1.0, 6.0, ((0, 4),), jnp.float32)
    ancestry = jnp.searchsorted(jnp.cumsum(ragged(key_list[2], K, NI, NI // 2, 2)), jnp.arange(NI), side="right").astype(jnp.int32)
    effects = scatter_about(key_list[3], (K, M), 0.5, 4.0, ((1, 8),), jnp.float32)
    prior_precision = draw_prior_precision(jax.random.fold_in(key_list[8], 71), 0)
    noise_var = jnp.clip(jnp.exp(jax.random.uniform(key_list[5], (K,), jnp.float32, math.log(0.5), math.log(2.0))), 0.5, 2.0)
    block_index = draw_block_index(jax.random.fold_in(key_list[8], 71), 0)
    gaussians = scatter_about(key_list[7], (STEPS, K, BLOCK), 1.0, 5.0, ((2, 8),), jnp.float32)
    return {"genotypes": genotypes, "residual": residual, "ancestry": ancestry, "effects": effects, "prior_precision": prior_precision, "noise_var": noise_var, "block_index": block_index, "gaussians": gaussians}


highest = lax.Precision.HIGHEST

def posterior_draw(scores, norm_sum, before, prior_precision, noise_var, noise_now):
    ancestries = scores.shape[0]
    inverse = 1.0 / noise_var
    target = (scores + norm_sum * before) * inverse[:, None]
    lower = [[None] * ancestries for column in range(ancestries)]
    for a in range(ancestries):
        for b in range(a + 1):
            total = prior_precision[a, b] + jnp.zeros_like(scores[0])
            if a == b:
                total = total + norm_sum[a] * inverse[a]
            for m in range(b):
                total = total - lower[a][m] * lower[b][m]
            if a == b:
                lower[a][a] = jnp.sqrt(total)
            else:
                lower[a][b] = total / lower[b][b]
    forward = []
    for a in range(ancestries):
        total = target[a]
        for m in range(a):
            total = total - lower[a][m] * forward[m]
        forward.append(total / lower[a][a] + noise_now[a])
    backward = [None] * ancestries
    for a in reversed(range(ancestries)):
        total = forward[a]
        for m in range(a + 1, ancestries):
            total = total - lower[m][a] * backward[m]
        backward[a] = total / lower[a][a]
    return jnp.stack(backward)

def reference(genotypes, residual, ancestry, effects, prior_precision, noise_var, block_index, gaussians):
    ancestries = effects.shape[0]
    onehot = (ancestry[None, :] == jnp.arange(ancestries, dtype=jnp.int32)[:, None]).astype(jnp.float32)
    offsets = (jnp.arange(BLOCK, dtype=jnp.int32) // BV * COLS).astype(jnp.int32)
    contract = (((1,), (1,)), ((), ()))
    for s in range(STEPS):
        picked = (block_index[s] + offsets).astype(jnp.int32)
        groups = picked.reshape(N_VAR, BV)
        weighted = onehot * residual[None, :]

        def score_group(indices):
            chosen = jnp.take(genotypes, indices, axis=0).astype(jnp.float32)
            first = lax.dot_general(weighted, chosen, contract, precision=highest)
            second = lax.dot_general(onehot, chosen * chosen, contract, precision=highest)
            return (first, second)
        scores, norm_sum = lax.map(score_group, groups)
        scores = scores.transpose(1, 0, 2).reshape(ancestries, BLOCK)
        norm_sum = norm_sum.transpose(1, 0, 2).reshape(ancestries, BLOCK)
        before = effects[:, picked]
        drawn = posterior_draw(scores, norm_sum, before, prior_precision, noise_var, gaussians[s])
        change = drawn - before
        effects = effects.at[:, picked].set(drawn)
        change_groups = change.reshape(ancestries, N_VAR, BV).transpose(1, 0, 2)

        def add_group(total, inputs):
            indices, delta = inputs
            chosen = jnp.take(genotypes, indices, axis=0).astype(jnp.float32)
            return (total + jnp.dot(delta, chosen, precision=highest), None)
        spread, unused = lax.scan(add_group, jnp.zeros((ancestries, NI), jnp.float32), (groups, change_groups))
        residual = residual - lax.optimization_barrier(jnp.sum(onehot * spread, axis=0))
    return (residual, effects)
```

```python
import functools

import jax
import jax.numpy as jnp
from jax import lax
from jax.experimental import pallas as pl
from jax.experimental.pallas import tpu as pltpu
from jax.sharding import PartitionSpec as P


LANES = 128
SUB = 8
ROWS = 16
GROUP = 8

f32, bf16 = jnp.float32, jnp.bfloat16
in_vmem = pl.BlockSpec(memory_space=pltpu.VMEM)
in_smem = pl.BlockSpec(memory_space=pltpu.SMEM)
in_hbm = pl.BlockSpec(memory_space=pl.ANY)


def split_rows(value):
    high = value.astype(bf16).astype(f32)
    return jnp.concatenate([high, value - high], axis=0).astype(bf16)


def row_of(ref, tile):
    return jnp.broadcast_to(ref[pl.ds(tile, 1), :], (SUB, LANES))


def group_scores(genotypes, residual, ancestry, column, tile, local):
    kind = lax.broadcasted_iota(jnp.int32, (SUB, LANES), 0)
    weights = []
    for t in range(GROUP):
        mine = row_of(ancestry, tile + t) == kind
        weights.append(split_rows(jnp.where(mine, row_of(residual, local + t), 0.0)))
    weights = jnp.concatenate(weights, axis=1)
    chosen = genotypes[:, pl.ds(column, GROUP * LANES)]
    return lax.dot_general(weights, chosen, (((1,), (1,)), ((), ())), preferred_element_type=f32)


def load_kernel(
    genotypes_hbm, residual, ancestry, block_index, gaussians,
    genotypes, payload, noise, picked, squares, semaphores,
):
    ancestries = squares.shape[0]
    tiles = residual.shape[0]
    chunks = semaphores.shape[0]
    per_chunk = tiles // chunks
    width = per_chunk * LANES

    def copy(i):
        part = pl.ds(pl.multiple_of(i * width, width), width)
        return pltpu.make_async_copy(genotypes_hbm.at[:, part], genotypes.at[:, part], semaphores.at[i])

    def start(i, carry):
        copy(i).start()
        return carry

    lax.fori_loop(0, chunks, start, 0)

    squares[...] = jnp.zeros_like(squares)
    lane = lax.broadcasted_iota(jnp.int32, (1, LANES), 1)
    for s in range(noise.shape[0]):
        def place(c, carry):
            hit = lane == block_index[s, c]
            rows = tuple(jnp.where(hit, gaussians[(s * ancestries + k), c], carry[k]) for k in range(ancestries))
            return rows + (jnp.where(hit, 1.0, carry[ancestries]),)

        empty = tuple(jnp.zeros((1, LANES), f32) for k in range(ancestries + 1))
        rows = lax.fori_loop(0, block_index.shape[1], place, empty)
        for k in range(ancestries):
            noise[s, pl.ds(k, 1), :] = rows[k]
        picked[pl.ds(s, 1), :] = rows[ancestries]

    below = []
    for k in range(1, ancestries):
        below.append(jnp.sum((ancestry[...] < k).astype(jnp.int32)))

    def at(column):
        return sum([(b <= column).astype(jnp.int32) for b in below])

    def chunk_step(i, scores):
        copy(i).wait()
        for g in range(per_chunk // GROUP):
            tile = i * per_chunk + g * GROUP
            column = pl.multiple_of(tile * LANES, GROUP * LANES)
            scores = scores + group_scores(genotypes, residual, ancestry, column, tile, tile)
        first, last = at(i * width), at(i * width + width - 1)

        def square_sum(k, masked):
            def body(g, sums):
                sums = list(sums)
                for t in range(2):
                    tile = i * per_chunk + g * 2 + t
                    column = pl.multiple_of(tile * LANES, LANES)
                    if masked:
                        mine = row_of(ancestry, tile) == k
                    for b in range(len(sums)):
                        x = genotypes[pl.ds(ROWS * b, ROWS), pl.ds(column, LANES)].astype(f32)
                        if masked:
                            x = jnp.where(jnp.concatenate([mine, mine], axis=0), x, 0.0)
                        sums[b] = sums[b] + x * x
                return tuple(sums)

            blocks = genotypes.shape[0] // ROWS
            zeros = tuple(jnp.zeros((ROWS, LANES), f32) for b in range(blocks))
            sums = lax.fori_loop(0, per_chunk // 2, body, zeros)
            for b in range(blocks):
                squares[k, pl.ds(ROWS * b, ROWS), :] += sums[b]

        @pl.when(first == last)
        def _():
            square_sum(first, False)

        @pl.when(first != last)
        def _():
            def one(k, carry):
                square_sum(k, True)
                return carry

            lax.fori_loop(first, last + 1, one, 0)

        return scores

    scores = lax.fori_loop(0, chunks, chunk_step, jnp.zeros((ROWS, genotypes.shape[0]), f32))
    payload[pl.ds(0, SUB), :] = scores[:SUB] + scores[SUB:]
    payload[pl.ds(SUB, SUB), :] = jnp.zeros((SUB, genotypes.shape[0]), f32)
    for k in range(ancestries):
        payload[pl.ds(SUB + k, 1), :] = jnp.sum(squares[k].T, axis=0, keepdims=True)


def tree_sum(values):
    while len(values) > 1:
        values = [values[i] + values[i + 1] for i in range(0, len(values), 2)]
    return values[0]


def cholesky(norms, prior, inverse, factor):
    ancestries = len(inverse)
    lower = {}
    for b in range(ancestries):
        for a in range(b, ancestries):
            total = prior[a, b] + jnp.zeros_like(norms[0])
            if a == b:
                total = total + norms[a] * inverse[a]
            for m in range(b):
                total = total - lower[a, m] * lower[b, m]
            if a == b:
                lower[a, a] = 1.0 / jnp.sqrt(total)
            else:
                lower[a, b] = total * lower[b, b]
            factor[pl.ds(a * ancestries + b, 1), :] = lower[a, b]


def draw_change(scores, norms, before, factor, inverse, noise, hit, effects_out, change):
    ancestries = len(inverse)
    low = lambda a, b: factor[pl.ds(a * ancestries + b, 1), :]
    forward = []
    for a in range(ancestries):
        total = (scores[a] + norms[a] * before[a]) * inverse[a]
        for m in range(a):
            total = total - low(a, m) * forward[m]
        forward.append(total * low(a, a) + noise[a])
    backward = [None] * ancestries
    for a in reversed(range(ancestries)):
        total = forward[a]
        for m in range(a + 1, ancestries):
            total = total - low(m, a) * backward[m]
        backward[a] = total * low(a, a)
    change[...] = jnp.zeros_like(change)
    for a in range(ancestries):
        effects_out[pl.ds(a, 1), :] = jnp.where(hit, backward[a], before[a])
        change[pl.ds(a, 1), :] = jnp.where(hit, backward[a] - before[a], 0.0)


def sublane_sums(tiles):
    row = lax.broadcasted_iota(jnp.int32, (SUB, LANES), 0)
    for half in (1, 2, 4):
        low = (row & half) == 0
        tiles = [
            jnp.where(low, a, b) + pltpu.roll(jnp.where(low, b, a), half, 0)
            for a, b in zip(tiles[::2], tiles[1::2])
        ]
    return tiles[0]


def draw_kernel(step, first, payloads, *refs):
    genotypes, ancestry, effects, prior, noise_var, noise, picked = refs[:7]
    parts = refs[7 : 7 + payloads]
    rest = refs[7 + payloads :]
    if not first:
        norms_ref, factor_ref = rest[:2]
        rest = rest[2:]
    keep, send, effects_out, norms_out, factor_out = rest[:5] if first else (*rest[:3], None, None)
    change = rest[-1]
    ancestries = effects.shape[0]
    inverse = [1.0 / noise_var[k] for k in range(ancestries)]
    total = tree_sum([part[...] for part in parts])
    if first:
        norms_out[...] = total[SUB:]
        norms = [norms_out[pl.ds(k, 1), :] for k in range(ancestries)]
        cholesky(norms, prior, inverse, factor_out)
        factor = factor_out
    else:
        norms = [norms_ref[pl.ds(k, 1), :] for k in range(ancestries)]
        factor = factor_ref
    scores = [total[k : k + 1] for k in range(ancestries)]
    before = [effects[pl.ds(k, 1), :] for k in range(ancestries)]
    noises = [noise[step, pl.ds(k, 1), :] for k in range(ancestries)]
    hit = picked[pl.ds(step, 1), :] > 0.5
    draw_change(scores, norms, before, factor, inverse, noises, hit, effects_out, change)

    weights = split_rows(change[...])
    kind = lax.broadcasted_iota(jnp.int32, (SUB, LANES), 0)
    me = lax.axis_index("var")
    pairs, per_part = keep.shape[0], keep.shape[1]
    for out, odd in ((send, 1), (keep, 0)):
        for pair in range(pairs):
            owner = me ^ (2 * pair + odd)

            def body(g, carry):
                tile = owner * per_part + g * GROUP
                column = pl.multiple_of(tile * LANES, GROUP * LANES)
                both = jnp.dot(
                    weights, genotypes[:, pl.ds(column, GROUP * LANES)], preferred_element_type=f32
                )
                both = both[:SUB] + both[SUB:]
                tiles = [
                    jnp.where(row_of(ancestry, tile + t) == kind, both[:, t * LANES : (t + 1) * LANES], 0.0)
                    for t in range(GROUP)
                ]
                out[pair, pl.ds(pl.multiple_of(g * GROUP, GROUP), GROUP), :] = sublane_sums(tiles)
                return carry

            lax.fori_loop(0, per_part // GROUP, body, 0)


def pair_kernel(keep, received, *outs):
    for pair, out in enumerate(outs):
        out[...] = keep[pair] + received[pair]


def chip_kernel(first, old, *refs):
    parts, out = refs[:-1], refs[-1]
    rows = out.shape[0]
    before = old[pl.ds(pl.multiple_of(lax.axis_index("var") * rows, SUB), rows), :] if first else old[...]
    out[...] = before - tree_sum([part[...] for part in parts])


def scores_kernel(offsets, genotypes, ancestry, *refs):
    parts, out = refs[:-1], refs[-1]
    me = lax.axis_index("var")
    rows = parts[0].shape[0]
    scores = jnp.zeros((ROWS, genotypes.shape[0]), f32)
    for offset, part in zip(offsets, parts):
        owner = me ^ offset

        def body(g, scores):
            tile = owner * rows + g * GROUP
            column = pl.multiple_of(tile * LANES, GROUP * LANES)
            return scores + group_scores(genotypes, part, ancestry, column, tile, g * GROUP)

        scores = lax.fori_loop(0, rows // GROUP, body, scores)
    out[...] = scores[:SUB] + scores[SUB:]


def resident(array):
    return pltpu.with_memory_space_constraint(array, pltpu.VMEM)


def params():
    return pltpu.CompilerParams(vmem_limit_bytes=8 << 20)


def exchange(array, axis, offset):
    size = lax.axis_size(axis)
    return lax.ppermute(array, axis, [(i, i ^ offset) for i in range(size)])


def gather_ind(array):
    parts, offset = [array], 1
    while offset < lax.axis_size("ind"):
        parts = parts + [exchange(part, "ind", offset) for part in parts]
        offset *= 2
    return parts


def per_device(
    genotypes, residual, ancestry, effects, prior_precision, noise_var, block_index, gaussians
):
    ancestries, variants = effects.shape
    steps = block_index.shape[0]
    people = residual.shape[0]
    var_size = lax.axis_size("var")
    chips = var_size // 2
    tiles = people // LANES
    rows = tiles // var_size
    per_chunk = 32
    while tiles % per_chunk:
        per_chunk //= 2
    residual = residual.reshape(tiles, LANES)
    ancestry = ancestry.reshape(tiles, LANES)
    shape = jax.ShapeDtypeStruct

    held, payload, noise, picked = pl.pallas_call(
        load_kernel,
        out_shape=(
            pltpu.VMEM(genotypes.shape, bf16),
            shape((ROWS, variants), f32),
            shape((steps, ancestries, variants), f32),
            shape((steps, variants), f32),
        ),
        in_specs=[in_hbm, in_vmem, in_vmem, in_smem, in_smem],
        out_specs=(in_vmem,) * 4,
        scratch_shapes=[
            pltpu.VMEM((ancestries, variants, LANES), f32),
            pltpu.SemaphoreType.DMA((tiles // per_chunk,)),
        ],
        compiler_params=params(),
        name="load",
    )(genotypes, residual, ancestry, block_index, gaussians.reshape(steps * ancestries, -1))

    current = residual
    norms = factor = None
    for s in range(steps):
        first = s == 0
        parts = gather_ind(payload)
        extra = [] if first else [norms, factor]
        part_shape = shape((chips, rows, LANES), f32)
        outs = [part_shape, part_shape, shape(effects.shape, f32)]
        if first:
            outs += [shape((SUB, variants), f32), shape((ancestries * ancestries, variants), f32)]
        results = pl.pallas_call(
            functools.partial(draw_kernel, s, first, len(parts)),
            out_shape=tuple(outs),
            in_specs=[in_vmem] * 3 + [in_smem] * 2 + [in_vmem] * (2 + len(parts) + len(extra)),
            out_specs=(in_vmem,) * len(outs),
            scratch_shapes=[pltpu.VMEM((SUB, variants), f32)],
            compiler_params=params(),
            name=f"draw{s}",
        )(resident(held), ancestry, effects, prior_precision, noise_var, noise, picked, *parts, *extra)
        keep, send, effects = results[:3]
        if first:
            norms, factor = results[3:]
        received = exchange(send, "var", 1)
        sums = pl.pallas_call(
            pair_kernel,
            out_shape=(shape((rows, LANES), f32),) * chips,
            in_specs=[in_vmem] * 2,
            out_specs=(in_vmem,) * chips,
            compiler_params=params(),
            name=f"pair{s}",
        )(keep, received)
        arrived = [sums[0]] + [exchange(sums[e], "var", 2 * e) for e in range(1, chips)]
        current = pl.pallas_call(
            functools.partial(chip_kernel, first),
            out_shape=shape((rows, LANES), f32),
            in_specs=[in_vmem] * (1 + chips),
            out_specs=in_vmem,
            compiler_params=params(),
            name=f"chip{s}",
        )(current, *arrived)
        if s + 1 == steps:
            break
        even = [current] + [exchange(current, "var", 2 * e) for e in range(1, chips)]
        odd = [exchange(part, "var", 1) for part in even]
        offsets = [2 * e for e in range(chips)] + [2 * e + 1 for e in range(chips)]
        payload = pl.pallas_call(
            functools.partial(scores_kernel, offsets),
            out_shape=shape((SUB, variants), f32),
            in_specs=[in_vmem] * (2 + var_size),
            out_specs=in_vmem,
            compiler_params=params(),
            name=f"scores{s}",
        )(resident(held), ancestry, *even, *odd)
    return current.reshape(-1), effects


def solution(mesh):
    return jax.shard_map(
        per_device,
        mesh=mesh,
        in_specs=(
            P("var", "ind"),
            P("ind"),
            P("ind"),
            P(None, "var"),
            P(),
            P(),
            P(None, "var"),
            P(None, None, "var"),
        ),
        out_specs=(P(("ind", "var")), P(None, "var")),
        check_vma=False,
    )
```

```python
import functools

import jax
import jax.numpy as jnp
from jax import lax
from jax.experimental import pallas as pl
from jax.experimental.pallas import tpu as pltpu
from jax.sharding import PartitionSpec as P


LANES = 128
SUB = 8
BLOCK = 8

f32, bf16, i32 = jnp.float32, jnp.bfloat16, jnp.int32
in_vmem = pl.BlockSpec(memory_space=pltpu.VMEM)
in_hbm = pl.BlockSpec(memory_space=pltpu.HBM)


def tile_lanes(tile, count=1):
    return pl.ds(pl.multiple_of(tile * LANES, count * LANES), count * LANES)


def row_of(ref, tile, rows):
    return jnp.broadcast_to(ref[pl.ds(tile, 1), :], (rows, LANES))


def lanes_iota(rows):
    return lax.broadcasted_iota(i32, (rows, LANES), 1)


def read_limits(limits, ancestries):
    return [limits[k, 0] for k in range(ancestries + 1)]


def ancestry_at(starts, column):
    return sum([(start <= column).astype(i32) for start in starts[1:-1]])


def pack_columns(columns):
    groups = columns[0].shape[0] // SUB
    stride = LANES // groups
    lane = lanes_iota(SUB)
    packed = jnp.zeros((SUB, LANES), f32)
    for k, column in enumerate(columns):
        for b in range(groups):
            packed = jnp.where(lane == stride * b + k, column[SUB * b : SUB * (b + 1)], packed)
    return packed


def pack_sums(sums):
    return pack_columns([jnp.sum(sums[k], axis=1, keepdims=True) for k in range(sums.shape[0])])


def unpack_column(packed, k, rows):
    stride = LANES // (rows // SUB)
    parts = [
        jnp.broadcast_to(packed[:, stride * b + k : stride * b + k + 1], (SUB, LANES))
        for b in range(rows // SUB)
    ]
    return jnp.concatenate(parts, axis=0)


def load_kernel(
    genotypes_hbm, residual_hbm, ancestry_hbm, index_hbm, prior_hbm, noise_var_hbm,
    rows_out, payload, limits, selected, consts,
    genotypes, residual, ancestry, index, prior, noise_var, squares, products, semaphores, small,
):
    ancestries, block, _ = products.shape
    total = rows_out.shape[0]
    steps = total // block
    tiles = residual.shape[0]
    chunks = semaphores.shape[0]
    per_chunk = tiles // chunks

    sources = (index_hbm, prior_hbm, noise_var_hbm, ancestry_hbm, residual_hbm)
    targets = (index, prior, noise_var, ancestry, residual)
    copies = [pltpu.make_async_copy(a, b, small.at[i]) for i, (a, b) in enumerate(zip(sources, targets))]
    for one in copies:
        one.start()

    def copy(i):
        part = tile_lanes(i * per_chunk, per_chunk)
        return pltpu.make_async_copy(genotypes_hbm.at[:, part], genotypes.at[:, part], semaphores.at[i])

    def start(i, carry):
        copy(i).start()
        return carry

    lax.fori_loop(0, chunks, start, 0)
    squares[...] = jnp.zeros_like(squares)
    products[...] = jnp.zeros_like(products)

    copies[0].wait()
    lane = lanes_iota(1)
    for s in range(steps):
        for c in range(block):
            selected[pl.ds(s * block + c, 1), :] = (lane == index[s, c]).astype(f32)
    copies[1].wait()
    copies[2].wait()
    for a in range(ancestries):
        for b in range(ancestries):
            consts[pl.ds(a * ancestries + b, 1), :] = jnp.full((1, LANES), prior[a, b], f32)
        row = ancestries * ancestries + a
        consts[pl.ds(row, 1), :] = 1.0 / jnp.full((1, LANES), noise_var[0, a], f32)

    copies[3].wait()
    starts = [0]
    for k in range(1, ancestries):
        starts.append(jnp.sum((ancestry[...] < k).astype(i32)))
    starts.append(tiles * LANES)
    for k, first in enumerate(starts):
        limits[pl.ds(k, 1), :] = jnp.full((1, LANES), first, i32)
    copies[4].wait()
    choose = selected[...].astype(bf16)

    def gather(tile):
        picked = jnp.dot(choose, genotypes[:, tile_lanes(tile, BLOCK)], preferred_element_type=f32)
        rows_out[:, tile_lanes(tile, BLOCK)] = picked.astype(bf16)
        return picked

    def chunk_step(i, carry):
        copy(i).wait()
        base = i * per_chunk
        low = ancestry_at(starts, base * LANES)
        high = ancestry_at(starts, (base + per_chunk) * LANES - 1)

        @pl.when(low == high)
        def _():
            square = jnp.zeros((block, LANES), f32)
            product = jnp.zeros((block, LANES), f32)
            for g in range(per_chunk // BLOCK):
                tile = base + g * BLOCK
                picked = gather(tile)
                for t in range(BLOCK):
                    x = picked[:block, t * LANES : (t + 1) * LANES]
                    square = square + x * x
                    product = product + x * row_of(residual, tile + t, block)
            squares[low] += square
            products[low] += product

        @pl.when(low != high)
        def _():
            def mixed(g, carry):
                tile = base + g * BLOCK
                gather(tile)

                def one(k, carry):
                    square = jnp.zeros((block, LANES), f32)
                    product = jnp.zeros((block, LANES), f32)
                    for t in range(BLOCK):
                        mine = row_of(ancestry, tile + t, block) == k
                        x = rows_out[pl.ds(0, block), tile_lanes(tile + t)].astype(f32)
                        x = jnp.where(mine, x, 0.0)
                        square = square + x * x
                        product = product + x * row_of(residual, tile + t, block)
                    squares[k] += square
                    products[k] += product
                    return carry

                first = ancestry_at(starts, tile * LANES)
                last = ancestry_at(starts, (tile + BLOCK) * LANES - 1)
                lax.fori_loop(first, last + 1, one, 0)
                return carry

            lax.fori_loop(0, per_chunk // BLOCK, mixed, 0)

        return carry

    lax.fori_loop(0, chunks, chunk_step, 0)
    payload[pl.ds(0, SUB), :] = pack_sums(products)
    payload[pl.ds(SUB, SUB), :] = pack_sums(squares)


def tree_sum(values):
    while len(values) > 1:
        values = [values[i] + values[i + 1] for i in range(0, len(values), 2)]
    return values[0]


def factor_columns(packed, before, consts, rows, store):
    ancestries = len(before)
    norms = [unpack_column(packed, k, rows) for k in range(ancestries)]
    const = lambda i: jnp.broadcast_to(consts[pl.ds(i, 1), :], (rows, LANES))
    lower = {}
    for b in range(ancestries):
        for a in range(b, ancestries):
            total = const(a * ancestries + b)
            if a == b:
                total = total + norms[a] * const(ancestries * ancestries + a)
            for m in range(b):
                total = total - lower[a, m] * lower[b, m]
            lower[a, b] = 1.0 / jnp.sqrt(total) if a == b else total * lower[b, b]
            store[a * ancestries + b] = lower[a, b]
    for k in range(ancestries):
        store[ancestries * ancestries + k] = norms[k] * before[k]


def commit(effects, selected, fresh, out):
    hit = selected > 0.5
    taken = jnp.sum(selected, axis=0, keepdims=True) > 0.5
    for k in range(out.shape[0]):
        value = jnp.sum(jnp.where(hit, fresh[k], 0.0), axis=0, keepdims=True)
        out[pl.ds(k, 1), :] = jnp.where(taken, value, effects[pl.ds(k, 1), :])


def prepare_kernel(step, *refs):
    selected, effects, gaussians = refs[:3]
    ancestries = effects.shape[0]
    rows = gaussians.shape[2]
    mine = lambda s: selected[pl.ds(s * rows, rows), :]
    if step == 0:
        columns = refs[3]
    else:
        fresh, columns, new_effects = refs[3:]
        commit(effects, mine(step - 1), fresh, new_effects)
        effects = new_effects
    hit = mine(step) > 0.5
    side = lax.broadcasted_iota(i32, (rows, rows), 0) == lax.broadcasted_iota(i32, (rows, rows), 1)
    for k in range(ancestries):
        noise = jnp.broadcast_to(gaussians[k, pl.ds(step, 1), :], (rows, rows))
        noise = jnp.sum(jnp.where(side, noise, 0.0), axis=1, keepdims=True)
        columns[k] = jnp.broadcast_to(noise, (rows, LANES))
        old = jnp.where(hit, row_of(effects, k, rows), 0.0)
        columns[ancestries + k] = jnp.broadcast_to(jnp.sum(old, axis=1, keepdims=True), (rows, LANES))


def commit_kernel(step, selected, effects, fresh, out):
    rows = fresh.shape[1]
    commit(effects, selected[pl.ds(step * rows, rows), :], fresh, out)


def sublane_sums(tiles):
    row = lax.broadcasted_iota(i32, (SUB, LANES), 0)
    for half in (1, 2, 4):
        low = (row & half) == 0
        tiles = [
            jnp.where(low, a, b) + pltpu.roll(jnp.where(low, b, a), half, 0)
            for a, b in zip(tiles[::2], tiles[1::2])
        ]
    return tiles[0]


def block_spread(rows_ref, step, change, tile):
    rows = change[0].shape[0] * len(change)
    tiles = []
    for t in range(BLOCK):
        x = rows_ref[pl.ds(step * rows, rows), tile_lanes(tile + t)].astype(f32)
        products = [x[SUB * b : SUB * (b + 1)] * c for b, c in enumerate(change)]
        tiles.append(tree_sum(products))
    return sublane_sums(tiles)


def group_size(tiles):
    size = 32
    while tiles % size:
        size //= 2
    return size


def spread_half(step, odd, rows_ref, limits, change_ref, out):
    ancestries, rows, _ = change_ref.shape
    starts = read_limits(limits, ancestries)
    me = lax.axis_index("var")
    pairs, per_part = out.shape[0], out.shape[1]
    group = group_size(per_part)
    change_of = lambda k: [change_ref[k, pl.ds(SUB * b, SUB), :] for b in range(rows // SUB)]

    def spread(i, carry):
        pair, local = i // (per_part // group), (i % (per_part // group)) * group
        base = (me ^ (2 * pair + odd)) * per_part + local
        first = ancestry_at(starts, base * LANES)
        last = ancestry_at(starts, (base + group) * LANES - 1)
        place = lambda g: pl.ds(pl.multiple_of(local + g * BLOCK, BLOCK), BLOCK)

        @pl.when(first == last)
        def _():
            change = change_of(first)
            for g in range(group // BLOCK):
                out[pair, place(g), :] = block_spread(rows_ref, step, change, base + g * BLOCK)

        @pl.when(first != last)
        def _():
            def mixed(g, carry):
                tile = base + g * BLOCK
                column = (tile + lax.broadcasted_iota(i32, (BLOCK, LANES), 0)) * LANES + lanes_iota(BLOCK)

                def one(k, value):
                    mine = block_spread(rows_ref, step, change_of(k), tile)
                    return jnp.where(column >= limits[k, 0], mine, value)

                begin = ancestry_at(starts, tile * LANES)
                end = ancestry_at(starts, (tile + BLOCK) * LANES - 1)
                out[pair, place(g), :] = lax.fori_loop(begin, end + 1, one, jnp.zeros((BLOCK, LANES), f32))
                return carry

            lax.fori_loop(0, group // BLOCK, mixed, 0)

        return carry

    lax.fori_loop(0, pairs * (per_part // group), spread, 0)


def draw_kernel(step, payloads, rows_ref, limits, columns, consts, *refs):
    parts = refs[:payloads]
    send, fresh_out, change_ref, factor = refs[payloads:]
    ancestries, rows, _ = fresh_out.shape
    total = tree_sum([part[...] for part in parts])
    noise = [columns[k] for k in range(ancestries)]
    before = [columns[ancestries + k] for k in range(ancestries)]
    factor_columns(total[SUB:], before, consts, rows, factor)
    low = lambda a, b: factor[a * ancestries + b]
    forward = []
    for a in range(ancestries):
        value = unpack_column(total[:SUB], a, rows) + factor[ancestries * ancestries + a]
        value = value * row_of(consts, ancestries * ancestries + a, rows)
        for m in range(a):
            value = value - low(a, m) * forward[m]
        forward.append(value * low(a, a) + noise[a])
    fresh = [None] * ancestries
    for a in reversed(range(ancestries)):
        value = forward[a]
        for m in range(a + 1, ancestries):
            value = value - low(m, a) * fresh[m]
        fresh[a] = value * low(a, a)
        fresh_out[a] = fresh[a]
        change_ref[a] = fresh[a] - before[a]
    spread_half(step, 1, rows_ref, limits, change_ref, send)


def keep_kernel(step, rows_ref, limits, change_ref, out):
    spread_half(step, 0, rows_ref, limits, change_ref, out)


def pair_kernel(keep, received, *outs):
    for pair, out in enumerate(outs):
        out[...] = keep[pair] + received[pair]


def chip_kernel(count, old, *refs):
    parts, out = refs[:count], refs[-1]
    out[...] = old[...] - tree_sum([part[...] for part in parts])


def own_kernel(residual_hbm, out, semaphore):
    rows = out.shape[0]
    mine = pl.ds(pl.multiple_of(lax.axis_index("var") * rows, SUB), rows)
    copy = pltpu.make_async_copy(residual_hbm.at[mine, :], out, semaphore)
    copy.start()
    copy.wait()


def segment_sums(step, rows_ref, limits, sums, tiles, base_of, residual=None):
    ancestries, rows, _ = sums.shape
    starts = read_limits(limits, ancestries)
    group = group_size(tiles)

    def body(i, carry):
        base = base_of(i * group)
        first = ancestry_at(starts, base * LANES)
        last = ancestry_at(starts, (base + group) * LANES - 1)

        def one(t, k=None):
            x = rows_ref[pl.ds(step * rows, rows), tile_lanes(base + t)].astype(f32)
            other = x if residual is None else row_of(residual, i * group + t, rows)
            if k is not None:
                column = (base + t) * LANES + lanes_iota(1)
                mine = (column >= limits[k, 0]) & (column < limits[k + 1, 0])
                x = jnp.where(jnp.broadcast_to(mine, x.shape), x, 0.0)
            return x * other

        @pl.when(first == last)
        def _():
            total = jnp.zeros((rows, LANES), f32)
            for t in range(group):
                total = total + one(t)
            sums[first] += total

        @pl.when(first != last)
        def _():
            def mixed(g, carry):
                def each(k, carry):
                    total = jnp.zeros((rows, LANES), f32)
                    for t in range(BLOCK):
                        total = total + one(g * BLOCK + t, k)
                    sums[k] += total
                    return carry

                begin = ancestry_at(starts, (base + g * BLOCK) * LANES)
                end = ancestry_at(starts, (base + (g + 1) * BLOCK) * LANES - 1)
                lax.fori_loop(begin, end + 1, each, 0)
                return carry

            lax.fori_loop(0, group // BLOCK, mixed, 0)

        return carry

    lax.fori_loop(0, residual.shape[0] // group if residual is not None else tiles // group, body, 0)


def norms_kernel(step, rows_ref, limits, out, sums):
    sums[...] = jnp.zeros_like(sums)
    tiles = rows_ref.shape[1] // LANES
    segment_sums(step, rows_ref, limits, sums, tiles, lambda local: local)
    out[...] = pack_sums(sums)


def scores_kernel(step, odd, count, rows_ref, limits, *refs):
    parts, rest = refs[:count], refs[count:]
    if odd:
        before, norms, out, residual, sums = rest
        sums[...] = before[...]
    else:
        sums, residual = rest
        sums[...] = jnp.zeros_like(sums)
    per_part = parts[0].shape[0]
    for p, part in enumerate(parts):
        residual[pl.ds(p * per_part, per_part), :] = part[...]
    me = lax.axis_index("var")
    base_of = lambda local: (me ^ (2 * (local // per_part) + odd)) * per_part + local % per_part
    segment_sums(step, rows_ref, limits, sums, per_part, base_of, residual)
    if odd:
        out[pl.ds(0, SUB), :] = pack_sums(sums)
        out[pl.ds(SUB, SUB), :] = norms[...]


def call(kernel, name, outs, inputs, scratch=(), limit=8, specs=None):
    return pl.pallas_call(
        kernel,
        out_shape=outs,
        in_specs=specs or [in_vmem] * len(inputs),
        out_specs=jax.tree.map(lambda out: in_vmem, outs),
        scratch_shapes=list(scratch),
        compiler_params=pltpu.CompilerParams(vmem_limit_bytes=limit << 20),
        name=name,
    )(*inputs)


def exchange(array, axis, offset):
    size = lax.axis_size(axis)
    return lax.ppermute(array, axis, [(i, i ^ offset) for i in range(size)])


def gather_ind(array):
    parts, offset = [array], 1
    while offset < lax.axis_size("ind"):
        parts = parts + [exchange(part, "ind", offset) for part in parts]
        offset *= 2
    return parts


def per_device(
    genotypes, residual, ancestry, effects, prior_precision, noise_var, block_index, gaussians
):
    ancestries, variants = effects.shape
    steps, block = block_index.shape
    people = residual.shape[0]
    var_size = lax.axis_size("var")
    chips = var_size // 2
    tiles = people // LANES
    part = tiles // var_size
    per_chunk = 64
    while tiles % per_chunk:
        per_chunk //= 2
    shape = jax.ShapeDtypeStruct
    in_place = lambda array: pltpu.with_memory_space_constraint(array, pltpu.HBM)
    residual = residual.reshape(tiles, LANES)
    ancestry = ancestry.reshape(tiles, LANES)
    noise_var = noise_var.reshape(1, ancestries)
    gaussians = gaussians.transpose(1, 0, 2)
    inputs = [genotypes, residual, ancestry, block_index, prior_precision, noise_var]

    held, payload, limits, selected, consts = call(
        load_kernel,
        "load",
        (
            pltpu.VMEM((steps * block, people), bf16),
            shape((2 * SUB, LANES), f32),
            shape((SUB, LANES), i32),
            shape((steps * block, variants), f32),
            shape((ancestries * (ancestries + 1), LANES), f32),
        ),
        [in_place(array) for array in inputs],
        [
            pltpu.VMEM(genotypes.shape, bf16),
            pltpu.VMEM(residual.shape, f32),
            pltpu.VMEM(ancestry.shape, i32),
            pltpu.SMEM(block_index.shape, i32),
            pltpu.SMEM(prior_precision.shape, f32),
            pltpu.SMEM(noise_var.shape, f32),
            pltpu.VMEM((ancestries, block, LANES), f32),
            pltpu.VMEM((ancestries, block, LANES), f32),
            pltpu.SemaphoreType.DMA((tiles // per_chunk,)),
            pltpu.SemaphoreType.DMA((5,)),
        ],
        32,
        [in_hbm] * len(inputs),
    )
    held = pltpu.with_memory_space_constraint(held, pltpu.VMEM)
    current = call(
        own_kernel, "own", shape((part, LANES), f32), [in_place(residual)], [pltpu.SemaphoreType.DMA], 8, [in_hbm]
    )

    columns_shape = shape((2 * ancestries, block, LANES), f32)
    column_shape = shape((ancestries, block, LANES), f32)
    part_shape = shape((chips, part, LANES), f32)
    effects_shape = shape(effects.shape, f32)
    factor = pltpu.VMEM((ancestries * (ancestries + 1), block, LANES), f32)
    sums_scratch = pltpu.VMEM(column_shape.shape, f32)
    residual_scratch = pltpu.VMEM((chips * part, LANES), f32)
    fresh = None
    for s in range(steps):
        if s == 0:
            columns = call(
                functools.partial(prepare_kernel, s), f"prepare{s}", columns_shape, [selected, effects, gaussians]
            )
        else:
            columns, effects = call(
                functools.partial(prepare_kernel, s),
                f"prepare{s}",
                (columns_shape, effects_shape),
                [selected, effects, gaussians, fresh],
            )
        parts = gather_ind(payload)
        send, fresh, change = call(
            functools.partial(draw_kernel, s, len(parts)),
            f"draw{s}",
            (part_shape, column_shape, column_shape),
            [held, limits, columns, consts, *parts],
            [factor],
        )
        received = exchange(send, "var", 1)
        keep = call(functools.partial(keep_kernel, s), f"keep{s}", part_shape, [held, limits, change])
        sums = call(pair_kernel, f"pair{s}", (shape((part, LANES), f32),) * chips, [keep, received])
        arrived = [sums[0]] + [exchange(sums[e], "var", 2 * e) for e in range(1, chips)]
        norms = []
        if s + 1 < steps:
            kernel = functools.partial(norms_kernel, s + 1)
            norms = [call(kernel, f"norms{s}", shape((SUB, LANES), f32), [held, limits], [sums_scratch])]
        kernel = functools.partial(chip_kernel, chips)
        current = call(kernel, f"chip{s}", shape((part, LANES), f32), [current, *arrived, *norms])
        if s + 1 == steps:
            effects = call(
                functools.partial(commit_kernel, s), "commit", effects_shape, [selected, effects, fresh]
            )
            break
        even = [current] + [exchange(current, "var", 2 * e) for e in range(1, chips)]
        odd = [exchange(one, "var", 1) for one in even]
        partial = call(
            functools.partial(scores_kernel, s + 1, 0, chips),
            f"even{s}",
            column_shape,
            [held, limits, *even],
            [residual_scratch],
        )
        payload = call(
            functools.partial(scores_kernel, s + 1, 1, chips),
            f"odd{s}",
            shape((2 * SUB, LANES), f32),
            [held, limits, *odd, partial, *norms],
            [residual_scratch, sums_scratch],
        )
    return current.reshape(-1), effects


def solution(mesh):
    return jax.shard_map(
        per_device,
        mesh=mesh,
        in_specs=(
            P("var", "ind"),
            P("ind"),
            P("ind"),
            P(None, "var"),
            P(),
            P(),
            P(None, "var"),
            P(None, None, "var"),
        ),
        out_specs=(P(("ind", "var")), P(None, "var")),
        check_vma=False,
    )
```

```python
import functools

import jax
import jax.numpy as jnp
from jax import lax
from jax.experimental import pallas as pl
from jax.experimental.pallas import tpu as pltpu
from jax.sharding import PartitionSpec as P


LANES = 128
SUB = 8
BLOCK = 8

f32, bf16, i32 = jnp.float32, jnp.bfloat16, jnp.int32
in_vmem = pl.BlockSpec(memory_space=pltpu.VMEM)
in_hbm = pl.BlockSpec(memory_space=pltpu.HBM)


def tile_lanes(tile, count=1):
    return pl.ds(pl.multiple_of(tile * LANES, count * LANES), count * LANES)


def row_of(ref, tile, rows):
    return jnp.broadcast_to(ref[pl.ds(tile, 1), :], (rows, LANES))


def lanes_iota(rows):
    return lax.broadcasted_iota(i32, (rows, LANES), 1)


def read_limits(limits, ancestries):
    return [limits[k, 0] for k in range(ancestries + 1)]


def ancestry_at(starts, column):
    return sum([(start <= column).astype(i32) for start in starts[1:-1]])


def pack_columns(columns):
    groups = columns[0].shape[0] // SUB
    stride = LANES // groups
    lane = lanes_iota(SUB)
    packed = jnp.zeros((SUB, LANES), f32)
    for k, column in enumerate(columns):
        for b in range(groups):
            packed = jnp.where(lane == stride * b + k, column[SUB * b : SUB * (b + 1)], packed)
    return packed


def pack_sums(sums):
    return pack_columns([jnp.sum(sums[k], axis=1, keepdims=True) for k in range(sums.shape[0])])


def unpack_column(packed, k, rows):
    stride = LANES // (rows // SUB)
    parts = [
        jnp.broadcast_to(packed[:, stride * b + k : stride * b + k + 1], (SUB, LANES))
        for b in range(rows // SUB)
    ]
    return jnp.concatenate(parts, axis=0)


def load_kernel(
    genotypes_hbm, residual_hbm, ancestry_hbm, index_hbm, prior_hbm, noise_var_hbm,
    rows_out, payload, limits, selected, consts, own,
    genotypes, residual, ancestry, index, prior, noise_var, squares, products, semaphores, small,
):
    ancestries, block, _ = products.shape
    total = rows_out.shape[0]
    steps = total // block
    tiles = residual.shape[0]
    chunks = semaphores.shape[0]
    per_chunk = tiles // chunks

    sources = (index_hbm, prior_hbm, noise_var_hbm, ancestry_hbm, residual_hbm)
    targets = (index, prior, noise_var, ancestry, residual)
    copies = [pltpu.make_async_copy(a, b, small.at[i]) for i, (a, b) in enumerate(zip(sources, targets))]
    for one in copies:
        one.start()

    def copy(i):
        part = tile_lanes(i * per_chunk, per_chunk)
        return pltpu.make_async_copy(genotypes_hbm.at[:, part], genotypes.at[:, part], semaphores.at[i])

    def start(i, carry):
        copy(i).start()
        return carry

    lax.fori_loop(0, chunks, start, 0)
    squares[...] = jnp.zeros_like(squares)
    products[...] = jnp.zeros_like(products)

    copies[0].wait()
    lane = lanes_iota(1)
    for s in range(steps):
        for c in range(block):
            selected[pl.ds(s * block + c, 1), :] = (lane == index[s, c]).astype(f32)
    copies[1].wait()
    copies[2].wait()
    for a in range(ancestries):
        for b in range(ancestries):
            consts[pl.ds(a * ancestries + b, 1), :] = jnp.full((1, LANES), prior[a, b], f32)
        row = ancestries * ancestries + a
        consts[pl.ds(row, 1), :] = 1.0 / jnp.full((1, LANES), noise_var[0, a], f32)

    copies[3].wait()
    starts = [0]
    for k in range(1, ancestries):
        starts.append(jnp.sum((ancestry[...] < k).astype(i32)))
    starts.append(tiles * LANES)
    for k, first in enumerate(starts):
        limits[pl.ds(k, 1), :] = jnp.full((1, LANES), first, i32)
    copies[4].wait()
    mine = pl.multiple_of(lax.axis_index("var") * own.shape[0], SUB)
    own[...] = residual[pl.ds(mine, own.shape[0]), :]
    choose = selected[...].astype(bf16)

    def gather(tile):
        picked = jnp.dot(choose, genotypes[:, tile_lanes(tile, BLOCK)], preferred_element_type=f32)
        rows_out[:, tile_lanes(tile, BLOCK)] = picked.astype(bf16)
        return picked

    def chunk_step(i, carry):
        copy(i).wait()
        base = i * per_chunk
        low = ancestry_at(starts, base * LANES)
        high = ancestry_at(starts, (base + per_chunk) * LANES - 1)

        @pl.when(low == high)
        def _():
            square = jnp.zeros((block, LANES), f32)
            product = jnp.zeros((block, LANES), f32)
            for g in range(per_chunk // BLOCK):
                tile = base + g * BLOCK
                picked = gather(tile)
                for t in range(BLOCK):
                    x = picked[:block, t * LANES : (t + 1) * LANES]
                    square = square + x * x
                    product = product + x * row_of(residual, tile + t, block)
            squares[low] += square
            products[low] += product

        @pl.when(low != high)
        def _():
            for g in range(per_chunk // BLOCK):
                gather(base + g * BLOCK)

            def mixed(g, carry):
                tile = base + g * BLOCK

                def one(k, carry):
                    square = jnp.zeros((block, LANES), f32)
                    product = jnp.zeros((block, LANES), f32)
                    for t in range(BLOCK):
                        mine = row_of(ancestry, tile + t, block) == k
                        x = rows_out[pl.ds(0, block), tile_lanes(tile + t)].astype(f32)
                        x = jnp.where(mine, x, 0.0)
                        square = square + x * x
                        product = product + x * row_of(residual, tile + t, block)
                    squares[k] += square
                    products[k] += product
                    return carry

                first = ancestry_at(starts, tile * LANES)
                last = ancestry_at(starts, (tile + BLOCK) * LANES - 1)
                lax.fori_loop(first, last + 1, one, 0)
                return carry

            lax.fori_loop(0, per_chunk // BLOCK, mixed, 0)

        return carry

    lax.fori_loop(0, chunks, chunk_step, 0)
    payload[pl.ds(0, SUB), :] = pack_sums(products)
    payload[pl.ds(SUB, SUB), :] = pack_sums(squares)


def tree_sum(values):
    while len(values) > 1:
        values = [values[i] + values[i + 1] for i in range(0, len(values), 2)]
    return values[0]


def factor_columns(packed, before, consts, rows, store):
    ancestries = len(before)
    norms = [unpack_column(packed, k, rows) for k in range(ancestries)]
    const = lambda i: jnp.broadcast_to(consts[pl.ds(i, 1), :], (rows, LANES))
    lower = {}
    for b in range(ancestries):
        for a in range(b, ancestries):
            total = const(a * ancestries + b)
            if a == b:
                total = total + norms[a] * const(ancestries * ancestries + a)
            for m in range(b):
                total = total - lower[a, m] * lower[b, m]
            lower[a, b] = 1.0 / jnp.sqrt(total) if a == b else total * lower[b, b]
            store[a * ancestries + b] = lower[a, b]
    for k in range(ancestries):
        store[ancestries * ancestries + k] = norms[k] * before[k]


def commit(effects, selected, fresh, out):
    hit = selected > 0.5
    taken = jnp.sum(selected, axis=0, keepdims=True) > 0.5
    for k in range(out.shape[0]):
        value = jnp.sum(jnp.where(hit, fresh[k], 0.0), axis=0, keepdims=True)
        out[pl.ds(k, 1), :] = jnp.where(taken, value, effects[pl.ds(k, 1), :])


def prepare_kernel(step, *refs):
    selected, effects, gaussians = refs[:3]
    ancestries = effects.shape[0]
    rows = gaussians.shape[2]
    mine = lambda s: selected[pl.ds(s * rows, rows), :]
    if step == 0:
        columns = refs[3]
    else:
        fresh, columns, new_effects = refs[3:]
        commit(effects, mine(step - 1), fresh, new_effects)
        effects = new_effects
    hit = mine(step) > 0.5
    side = lax.broadcasted_iota(i32, (rows, rows), 0) == lax.broadcasted_iota(i32, (rows, rows), 1)
    for k in range(ancestries):
        noise = jnp.broadcast_to(gaussians[k, pl.ds(step, 1), :], (rows, rows))
        noise = jnp.sum(jnp.where(side, noise, 0.0), axis=1, keepdims=True)
        columns[k] = jnp.broadcast_to(noise, (rows, LANES))
        old = jnp.where(hit, row_of(effects, k, rows), 0.0)
        columns[ancestries + k] = jnp.broadcast_to(jnp.sum(old, axis=1, keepdims=True), (rows, LANES))


def commit_kernel(step, selected, effects, fresh, out):
    rows = fresh.shape[1]
    commit(effects, selected[pl.ds(step * rows, rows), :], fresh, out)


def sublane_sums(tiles):
    row = lax.broadcasted_iota(i32, (SUB, LANES), 0)
    for half in (1, 2, 4):
        low = (row & half) == 0
        tiles = [
            jnp.where(low, a, b) + pltpu.roll(jnp.where(low, b, a), half, 0)
            for a, b in zip(tiles[::2], tiles[1::2])
        ]
    return tiles[0]


def block_spread(rows_ref, step, change, tile):
    rows = change[0].shape[0] * len(change)
    tiles = []
    for t in range(BLOCK):
        x = rows_ref[pl.ds(step * rows, rows), tile_lanes(tile + t)].astype(f32)
        products = [x[SUB * b : SUB * (b + 1)] * c for b, c in enumerate(change)]
        tiles.append(tree_sum(products))
    return sublane_sums(tiles)


def group_size(tiles):
    size = 32
    while tiles % size:
        size //= 2
    return size


def spread_half(step, odd, rows_ref, limits, change_ref, out):
    ancestries, rows, _ = change_ref.shape
    starts = read_limits(limits, ancestries)
    me = lax.axis_index("var")
    pairs, per_part = out.shape[0], out.shape[1]
    group = group_size(per_part)
    change_of = lambda k: [change_ref[k, pl.ds(SUB * b, SUB), :] for b in range(rows // SUB)]

    def spread(i, carry):
        pair, local = i // (per_part // group), (i % (per_part // group)) * group
        base = (me ^ (2 * pair + odd)) * per_part + local
        first = ancestry_at(starts, base * LANES)
        last = ancestry_at(starts, (base + group) * LANES - 1)
        place = lambda g: pl.ds(pl.multiple_of(local + g * BLOCK, BLOCK), BLOCK)

        @pl.when(first == last)
        def _():
            change = change_of(first)
            for g in range(group // BLOCK):
                out[pair, place(g), :] = block_spread(rows_ref, step, change, base + g * BLOCK)

        @pl.when(first != last)
        def _():
            def mixed(g, carry):
                tile = base + g * BLOCK
                column = (tile + lax.broadcasted_iota(i32, (BLOCK, LANES), 0)) * LANES + lanes_iota(BLOCK)

                def one(k, value):
                    mine = block_spread(rows_ref, step, change_of(k), tile)
                    return jnp.where(column >= limits[k, 0], mine, value)

                begin = ancestry_at(starts, tile * LANES)
                end = ancestry_at(starts, (tile + BLOCK) * LANES - 1)
                out[pair, place(g), :] = lax.fori_loop(begin, end + 1, one, jnp.zeros((BLOCK, LANES), f32))
                return carry

            lax.fori_loop(0, group // BLOCK, mixed, 0)

        return carry

    lax.fori_loop(0, pairs * (per_part // group), spread, 0)


def draw_kernel(step, payloads, rows_ref, limits, columns, consts, *refs):
    parts = refs[:payloads]
    send, fresh_out, change_ref, factor = refs[payloads:]
    ancestries, rows, _ = fresh_out.shape
    total = tree_sum([part[...] for part in parts])
    noise = [columns[k] for k in range(ancestries)]
    before = [columns[ancestries + k] for k in range(ancestries)]
    factor_columns(total[SUB:], before, consts, rows, factor)
    low = lambda a, b: factor[a * ancestries + b]
    forward = []
    for a in range(ancestries):
        value = unpack_column(total[:SUB], a, rows) + factor[ancestries * ancestries + a]
        value = value * row_of(consts, ancestries * ancestries + a, rows)
        for m in range(a):
            value = value - low(a, m) * forward[m]
        forward.append(value * low(a, a) + noise[a])
    fresh = [None] * ancestries
    for a in reversed(range(ancestries)):
        value = forward[a]
        for m in range(a + 1, ancestries):
            value = value - low(m, a) * fresh[m]
        fresh[a] = value * low(a, a)
        fresh_out[a] = fresh[a]
        change_ref[a] = fresh[a] - before[a]
    spread_half(step, 1, rows_ref, limits, change_ref, send)


def keep_kernel(step, rows_ref, limits, change_ref, out):
    spread_half(step, 0, rows_ref, limits, change_ref, out)


def pair_kernel(keep, received, *outs):
    for pair, out in enumerate(outs):
        out[...] = keep[pair] + received[pair]


def chip_kernel(count, old, *refs):
    parts, out = refs[:count], refs[-1]
    out[...] = old[...] - tree_sum([part[...] for part in parts])


def segment_sums(step, rows_ref, limits, sums, tiles, base_of, residual=None):
    ancestries, rows, _ = sums.shape
    starts = read_limits(limits, ancestries)
    group = group_size(tiles)

    def body(i, carry):
        base = base_of(i * group)
        first = ancestry_at(starts, base * LANES)
        last = ancestry_at(starts, (base + group) * LANES - 1)

        def one(t, k=None):
            x = rows_ref[pl.ds(step * rows, rows), tile_lanes(base + t)].astype(f32)
            other = x if residual is None else row_of(residual, i * group + t, rows)
            if k is not None:
                column = (base + t) * LANES + lanes_iota(1)
                mine = (column >= limits[k, 0]) & (column < limits[k + 1, 0])
                x = jnp.where(jnp.broadcast_to(mine, x.shape), x, 0.0)
            return x * other

        @pl.when(first == last)
        def _():
            total = jnp.zeros((rows, LANES), f32)
            for t in range(group):
                total = total + one(t)
            sums[first] += total

        @pl.when(first != last)
        def _():
            def mixed(g, carry):
                def each(k, carry):
                    total = jnp.zeros((rows, LANES), f32)
                    for t in range(BLOCK):
                        total = total + one(g * BLOCK + t, k)
                    sums[k] += total
                    return carry

                begin = ancestry_at(starts, (base + g * BLOCK) * LANES)
                end = ancestry_at(starts, (base + (g + 1) * BLOCK) * LANES - 1)
                lax.fori_loop(begin, end + 1, each, 0)
                return carry

            lax.fori_loop(0, group // BLOCK, mixed, 0)

        return carry

    lax.fori_loop(0, residual.shape[0] // group if residual is not None else tiles // group, body, 0)


def norms_kernel(step, rows_ref, limits, out, sums):
    sums[...] = jnp.zeros_like(sums)
    tiles = rows_ref.shape[1] // LANES
    segment_sums(step, rows_ref, limits, sums, tiles, lambda local: local)
    out[...] = pack_sums(sums)


def scores_kernel(step, count, scale, shift, first, last, rows_ref, limits, *refs):
    parts, rest = refs[:count], refs[count:]
    residual = rest[-1] if not last else rest[-2]
    sums = rest[-2] if not last else rest[-1]
    sums[...] = jnp.zeros_like(sums) if first else rest[0][...]
    per_part = parts[0].shape[0]
    for p, part in enumerate(parts):
        residual[pl.ds(p * per_part, per_part), :] = part[...]
    me = lax.axis_index("var")
    base_of = lambda local: (me ^ (scale * (local // per_part) + shift)) * per_part + local % per_part
    segment_sums(step, rows_ref, limits, sums, per_part, base_of, residual)
    if last:
        norms, out = rest[1:3]
        out[pl.ds(0, SUB), :] = pack_sums(sums)
        out[pl.ds(SUB, SUB), :] = norms[...]


def call(kernel, outs, inputs, scratch=(), limit=8, specs=None):
    return pl.pallas_call(
        kernel,
        out_shape=outs,
        in_specs=specs or [in_vmem] * len(inputs),
        out_specs=jax.tree.map(lambda out: in_vmem, outs),
        scratch_shapes=list(scratch),
        compiler_params=pltpu.CompilerParams(vmem_limit_bytes=limit << 20),
    )(*inputs)


def exchange(array, axis, offset):
    size = lax.axis_size(axis)
    return lax.ppermute(array, axis, [(i, i ^ offset) for i in range(size)])


def gather_ind(array):
    parts, offset = [array], 1
    while offset < lax.axis_size("ind"):
        parts = parts + [exchange(part, "ind", offset) for part in parts]
        offset *= 2
    return parts


def update(
    genotypes, residual, ancestry, effects, prior_precision, noise_var, block_index, gaussians
):
    ancestries, variants = effects.shape
    steps, block = block_index.shape
    people = residual.shape[0]
    var_size = lax.axis_size("var")
    chips = var_size // 2
    tiles = people // LANES
    part = tiles // var_size
    per_chunk = 64
    while tiles % per_chunk:
        per_chunk //= 2
    shape = jax.ShapeDtypeStruct
    in_place = lambda array: pltpu.with_memory_space_constraint(array, pltpu.HBM)
    residual = residual.reshape(tiles, LANES)
    ancestry = ancestry.reshape(tiles, LANES)
    noise_var = noise_var.reshape(1, ancestries)
    gaussians = gaussians.transpose(1, 0, 2)
    inputs = [genotypes, residual, ancestry, block_index, prior_precision, noise_var]

    held, payload, limits, selected, consts, current = call(
        load_kernel,
        (
            pltpu.VMEM((steps * block, people), bf16),
            shape((2 * SUB, LANES), f32),
            shape((SUB, LANES), i32),
            shape((steps * block, variants), f32),
            shape((ancestries * (ancestries + 1), LANES), f32),
            shape((part, LANES), f32),
        ),
        [in_place(array) for array in inputs],
        [
            pltpu.VMEM(genotypes.shape, bf16),
            pltpu.VMEM(residual.shape, f32),
            pltpu.VMEM(ancestry.shape, i32),
            pltpu.SMEM(block_index.shape, i32),
            pltpu.SMEM(prior_precision.shape, f32),
            pltpu.SMEM(noise_var.shape, f32),
            pltpu.VMEM((ancestries, block, LANES), f32),
            pltpu.VMEM((ancestries, block, LANES), f32),
            pltpu.SemaphoreType.DMA((tiles // per_chunk,)),
            pltpu.SemaphoreType.DMA((5,)),
        ],
        32,
        [in_hbm] * len(inputs),
    )
    held = pltpu.with_memory_space_constraint(held, pltpu.VMEM)

    columns_shape = shape((2 * ancestries, block, LANES), f32)
    column_shape = shape((ancestries, block, LANES), f32)
    part_shape = shape((chips, part, LANES), f32)
    effects_shape = shape(effects.shape, f32)
    factor = pltpu.VMEM((ancestries * (ancestries + 1), block, LANES), f32)
    sums_scratch = pltpu.VMEM(column_shape.shape, f32)
    residual_scratch = pltpu.VMEM(((chips - 1) * part, LANES), f32)
    fresh = None
    for s in range(steps):
        if s == 0:
            columns = call(functools.partial(prepare_kernel, s), columns_shape, [selected, effects, gaussians])
        else:
            columns, effects = call(
                functools.partial(prepare_kernel, s),
                (columns_shape, effects_shape),
                [selected, effects, gaussians, fresh],
            )
        parts = gather_ind(payload)
        send, fresh, change = call(
            functools.partial(draw_kernel, s, len(parts)),
            (part_shape, column_shape, column_shape),
            [held, limits, columns, consts, *parts],
            [factor],
        )
        received = exchange(send, "var", 1)
        keep = call(functools.partial(keep_kernel, s), part_shape, [held, limits, change])
        sums = call(pair_kernel, (shape((part, LANES), f32),) * chips, [keep, received])
        arrived = [sums[0]] + [exchange(sums[e], "var", 2 * e) for e in range(1, chips)]
        norms = []
        if s + 1 < steps:
            kernel = functools.partial(norms_kernel, s + 1)
            norms = [call(kernel, shape((SUB, LANES), f32), [held, limits], [sums_scratch])]
        kernel = functools.partial(chip_kernel, chips)
        current = call(kernel, shape((part, LANES), f32), [current, *arrived, *norms])
        if s + 1 == steps:
            effects = call(functools.partial(commit_kernel, s), effects_shape, [selected, effects, fresh])
            break
        even = [current] + [exchange(current, "var", 2 * e) for e in range(1, chips)]
        odd = [exchange(one, "var", 1) for one in even]
        scores = functools.partial(scores_kernel, s + 1)
        partial = call(
            functools.partial(scores, 2, 1, 0, True, False),
            column_shape,
            [held, limits, even[0], odd[0]],
            [pltpu.VMEM((2 * part, LANES), f32)],
        )
        partial = call(
            functools.partial(scores, chips - 1, 2, 2, False, False),
            column_shape,
            [held, limits, *even[1:], partial],
            [residual_scratch],
        )
        payload = call(
            functools.partial(scores, chips - 1, 2, 3, False, True),
            shape((2 * SUB, LANES), f32),
            [held, limits, *odd[1:], partial, *norms],
            [residual_scratch, sums_scratch],
        )
    return current.reshape(-1), effects


def solution(mesh):
    return jax.shard_map(
        update,
        mesh=mesh,
        in_specs=(
            P("var", "ind"),
            P("ind"),
            P("ind"),
            P(None, "var"),
            P(),
            P(),
            P(None, "var"),
            P(None, None, "var"),
        ),
        out_specs=(P(("ind", "var")), P(None, "var")),
        check_vma=False,
    )
```

```python
import functools

import jax
import jax.numpy as jnp
from jax import lax
from jax.experimental import pallas as pl
from jax.experimental.pallas import tpu as pltpu
from jax.sharding import PartitionSpec as P


LANES = 128
SUB = 8
BLOCK = 8

f32, bf16, i32 = jnp.float32, jnp.bfloat16, jnp.int32
in_vmem = pl.BlockSpec(memory_space=pltpu.VMEM)
in_hbm = pl.BlockSpec(memory_space=pltpu.HBM)


def tile_lanes(tile, count=1):
    return pl.ds(pl.multiple_of(tile * LANES, count * LANES), count * LANES)


def row_of(ref, tile, rows):
    return jnp.broadcast_to(ref[pl.ds(tile, 1), :], (rows, LANES))


def lanes_iota(rows):
    return lax.broadcasted_iota(i32, (rows, LANES), 1)


def read_limits(limits, ancestries):
    return [limits[k, 0] for k in range(ancestries + 1)]


def ancestry_at(starts, column):
    return sum([(start <= column).astype(i32) for start in starts[1:-1]])


def pack_columns(columns):
    groups = columns[0].shape[0] // SUB
    stride = LANES // groups
    lane = lanes_iota(SUB)
    packed = jnp.zeros((SUB, LANES), f32)
    for k, column in enumerate(columns):
        for b in range(groups):
            packed = jnp.where(lane == stride * b + k, column[SUB * b : SUB * (b + 1)], packed)
    return packed


def pack_sums(sums):
    return pack_columns([jnp.sum(sums[k], axis=1, keepdims=True) for k in range(sums.shape[0])])


def unpack_column(packed, k, rows):
    stride = LANES // (rows // SUB)
    parts = [
        jnp.broadcast_to(packed[:, stride * b + k : stride * b + k + 1], (SUB, LANES))
        for b in range(rows // SUB)
    ]
    return jnp.concatenate(parts, axis=0)


def load_kernel(
    genotypes_hbm, residual_hbm, ancestry_hbm, index_hbm, prior_hbm, noise_var_hbm,
    rows_out, payload, limits, selected, consts, own,
    genotypes, residual, ancestry, index, prior, noise_var, squares, products, semaphores, small,
):
    ancestries, block, _ = products.shape
    total = rows_out.shape[0]
    steps = total // block
    tiles = residual.shape[0]
    chunks = semaphores.shape[0]
    per_chunk = tiles // chunks

    sources = (index_hbm, prior_hbm, noise_var_hbm, ancestry_hbm, residual_hbm)
    targets = (index, prior, noise_var, ancestry, residual)
    copies = [pltpu.make_async_copy(a, b, small.at[i]) for i, (a, b) in enumerate(zip(sources, targets))]
    for one in copies:
        one.start()

    def copy(i):
        part = tile_lanes(i * per_chunk, per_chunk)
        return pltpu.make_async_copy(genotypes_hbm.at[:, part], genotypes.at[:, part], semaphores.at[i])

    def start(i, carry):
        copy(i).start()
        return carry

    lax.fori_loop(0, chunks, start, 0)
    squares[...] = jnp.zeros_like(squares)
    products[...] = jnp.zeros_like(products)

    copies[0].wait()
    lane = lanes_iota(1)
    for s in range(steps):
        for c in range(block):
            selected[pl.ds(s * block + c, 1), :] = (lane == index[s, c]).astype(f32)
    copies[1].wait()
    copies[2].wait()
    for a in range(ancestries):
        for b in range(ancestries):
            consts[pl.ds(a * ancestries + b, 1), :] = jnp.full((1, LANES), prior[a, b], f32)
        row = ancestries * ancestries + a
        consts[pl.ds(row, 1), :] = 1.0 / jnp.full((1, LANES), noise_var[0, a], f32)

    copies[3].wait()
    starts = [0]
    for k in range(1, ancestries):
        starts.append(jnp.sum((ancestry[...] < k).astype(i32)))
    starts.append(tiles * LANES)
    for k, first in enumerate(starts):
        limits[pl.ds(k, 1), :] = jnp.full((1, LANES), first, i32)
    copies[4].wait()
    mine = pl.multiple_of(lax.axis_index("var") * own.shape[0], SUB)
    own[...] = residual[pl.ds(mine, own.shape[0]), :]
    choose = selected[...].astype(bf16)

    def gather(tile):
        picked = jnp.dot(choose, genotypes[:, tile_lanes(tile, BLOCK)], preferred_element_type=f32)
        rows_out[:, tile_lanes(tile, BLOCK)] = picked.astype(bf16)
        return picked

    def chunk_step(i, carry):
        copy(i).wait()
        base = i * per_chunk
        low = ancestry_at(starts, base * LANES)
        high = ancestry_at(starts, (base + per_chunk) * LANES - 1)

        @pl.when(low == high)
        def _():
            square = jnp.zeros((block, LANES), f32)
            product = jnp.zeros((block, LANES), f32)
            for g in range(per_chunk // BLOCK):
                tile = base + g * BLOCK
                picked = gather(tile)
                for t in range(BLOCK):
                    x = picked[:block, t * LANES : (t + 1) * LANES]
                    square = square + x * x
                    product = product + x * row_of(residual, tile + t, block)
            squares[low] += square
            products[low] += product

        @pl.when(low != high)
        def _():
            for g in range(per_chunk // BLOCK):
                gather(base + g * BLOCK)

            def mixed(g, carry):
                tile = base + g * BLOCK

                def one(k, carry):
                    square = jnp.zeros((block, LANES), f32)
                    product = jnp.zeros((block, LANES), f32)
                    for t in range(BLOCK):
                        mine = row_of(ancestry, tile + t, block) == k
                        x = rows_out[pl.ds(0, block), tile_lanes(tile + t)].astype(f32)
                        x = jnp.where(mine, x, 0.0)
                        square = square + x * x
                        product = product + x * row_of(residual, tile + t, block)
                    squares[k] += square
                    products[k] += product
                    return carry

                first = ancestry_at(starts, tile * LANES)
                last = ancestry_at(starts, (tile + BLOCK) * LANES - 1)
                lax.fori_loop(first, last + 1, one, 0)
                return carry

            lax.fori_loop(0, per_chunk // BLOCK, mixed, 0)

        return carry

    lax.fori_loop(0, chunks, chunk_step, 0)
    payload[pl.ds(0, SUB), :] = pack_sums(products)
    payload[pl.ds(SUB, SUB), :] = pack_sums(squares)


def tree_sum(values):
    while len(values) > 1:
        values = [values[i] + values[i + 1] for i in range(0, len(values), 2)]
    return values[0]


def factor_columns(packed, before, consts, rows, store):
    ancestries = len(before)
    norms = [unpack_column(packed, k, rows) for k in range(ancestries)]
    const = lambda i: jnp.broadcast_to(consts[pl.ds(i, 1), :], (rows, LANES))
    lower = {}
    for b in range(ancestries):
        for a in range(b, ancestries):
            total = const(a * ancestries + b)
            if a == b:
                total = total + norms[a] * const(ancestries * ancestries + a)
            for m in range(b):
                total = total - lower[a, m] * lower[b, m]
            lower[a, b] = 1.0 / jnp.sqrt(total) if a == b else total * lower[b, b]
            store[a * ancestries + b] = lower[a, b]
    for k in range(ancestries):
        store[ancestries * ancestries + k] = norms[k] * before[k]


def commit(effects, selected, fresh, out):
    hit = selected > 0.5
    taken = jnp.sum(selected, axis=0, keepdims=True) > 0.5
    for k in range(out.shape[0]):
        value = jnp.sum(jnp.where(hit, fresh[k], 0.0), axis=0, keepdims=True)
        out[pl.ds(k, 1), :] = jnp.where(taken, value, effects[pl.ds(k, 1), :])


def prepare_kernel(step, *refs):
    selected, effects, gaussians = refs[:3]
    ancestries = effects.shape[0]
    rows = gaussians.shape[2]
    mine = lambda s: selected[pl.ds(s * rows, rows), :]
    if step == 0:
        columns = refs[3]
    else:
        fresh, columns, new_effects = refs[3:]
        commit(effects, mine(step - 1), fresh, new_effects)
        effects = new_effects
    hit = mine(step) > 0.5
    side = lax.broadcasted_iota(i32, (rows, rows), 0) == lax.broadcasted_iota(i32, (rows, rows), 1)
    for k in range(ancestries):
        noise = jnp.broadcast_to(gaussians[k, pl.ds(step, 1), :], (rows, rows))
        noise = jnp.sum(jnp.where(side, noise, 0.0), axis=1, keepdims=True)
        columns[k] = jnp.broadcast_to(noise, (rows, LANES))
        old = jnp.where(hit, row_of(effects, k, rows), 0.0)
        columns[ancestries + k] = jnp.broadcast_to(jnp.sum(old, axis=1, keepdims=True), (rows, LANES))


def commit_kernel(step, selected, effects, fresh, out):
    rows = fresh.shape[1]
    commit(effects, selected[pl.ds(step * rows, rows), :], fresh, out)


def sublane_sums(tiles):
    row = lax.broadcasted_iota(i32, (SUB, LANES), 0)
    for half in (1, 2, 4):
        low = (row & half) == 0
        tiles = [
            jnp.where(low, a, b) + pltpu.roll(jnp.where(low, b, a), half, 0)
            for a, b in zip(tiles[::2], tiles[1::2])
        ]
    return tiles[0]


def block_spread(rows_ref, step, change, tile):
    rows = change[0].shape[0] * len(change)
    tiles = []
    for t in range(BLOCK):
        x = rows_ref[pl.ds(step * rows, rows), tile_lanes(tile + t)].astype(f32)
        products = [x[SUB * b : SUB * (b + 1)] * c for b, c in enumerate(change)]
        tiles.append(tree_sum(products))
    return sublane_sums(tiles)


def group_size(tiles):
    return next(size for size in (48, 32, 16, BLOCK) if tiles % size == 0)


def spread_half(step, odd, rows_ref, limits, change_ref, out):
    ancestries, rows, _ = change_ref.shape
    starts = read_limits(limits, ancestries)
    me = lax.axis_index("var")
    pairs, per_part = out.shape[0], out.shape[1]
    group = group_size(per_part)
    change_of = lambda k: [change_ref[k, pl.ds(SUB * b, SUB), :] for b in range(rows // SUB)]

    def spread(i, carry):
        pair, local = i // (per_part // group), (i % (per_part // group)) * group
        base = (me ^ (2 * pair + odd)) * per_part + local
        first = ancestry_at(starts, base * LANES)
        last = ancestry_at(starts, (base + group) * LANES - 1)
        place = lambda g: pl.ds(pl.multiple_of(local + g * BLOCK, BLOCK), BLOCK)

        @pl.when(first == last)
        def _():
            change = change_of(first)
            for g in range(group // BLOCK):
                out[pair, place(g), :] = block_spread(rows_ref, step, change, base + g * BLOCK)

        @pl.when(first != last)
        def _():
            def mixed(g, carry):
                tile = base + g * BLOCK
                column = (tile + lax.broadcasted_iota(i32, (BLOCK, LANES), 0)) * LANES + lanes_iota(BLOCK)

                def one(k, value):
                    mine = block_spread(rows_ref, step, change_of(k), tile)
                    return jnp.where(column >= limits[k, 0], mine, value)

                begin = ancestry_at(starts, tile * LANES)
                end = ancestry_at(starts, (tile + BLOCK) * LANES - 1)
                out[pair, place(g), :] = lax.fori_loop(begin, end + 1, one, jnp.zeros((BLOCK, LANES), f32))
                return carry

            lax.fori_loop(0, group // BLOCK, mixed, 0)

        return carry

    lax.fori_loop(0, pairs * (per_part // group), spread, 0)


def draw_kernel(step, payloads, rows_ref, limits, columns, consts, *refs):
    parts = refs[:payloads]
    send, fresh_out, change_ref, factor = refs[payloads:]
    ancestries, rows, _ = fresh_out.shape
    total = tree_sum([part[...] for part in parts])
    noise = [columns[k] for k in range(ancestries)]
    before = [columns[ancestries + k] for k in range(ancestries)]
    factor_columns(total[SUB:], before, consts, rows, factor)
    low = lambda a, b: factor[a * ancestries + b]
    forward = []
    for a in range(ancestries):
        value = unpack_column(total[:SUB], a, rows) + factor[ancestries * ancestries + a]
        value = value * row_of(consts, ancestries * ancestries + a, rows)
        for m in range(a):
            value = value - low(a, m) * forward[m]
        forward.append(value * low(a, a) + noise[a])
    fresh = [None] * ancestries
    for a in reversed(range(ancestries)):
        value = forward[a]
        for m in range(a + 1, ancestries):
            value = value - low(m, a) * fresh[m]
        fresh[a] = value * low(a, a)
        fresh_out[a] = fresh[a]
        change_ref[a] = fresh[a] - before[a]
    spread_half(step, 1, rows_ref, limits, change_ref, send)


def keep_kernel(step, rows_ref, limits, change_ref, out):
    spread_half(step, 0, rows_ref, limits, change_ref, out)


def pair_kernel(keep, received, *outs):
    for pair, out in enumerate(outs):
        out[...] = keep[pair] + received[pair]


def chip_kernel(count, old, *refs):
    parts, out = refs[:count], refs[-1]
    out[...] = old[...] - tree_sum([part[...] for part in parts])


def segment_sums(step, rows_ref, limits, sums, tiles, base_of, residual=None):
    ancestries, rows, _ = sums.shape
    starts = read_limits(limits, ancestries)
    group = group_size(tiles)

    def body(i, carry):
        base = base_of(i * group)
        first = ancestry_at(starts, base * LANES)
        last = ancestry_at(starts, (base + group) * LANES - 1)

        def one(t, k=None):
            x = rows_ref[pl.ds(step * rows, rows), tile_lanes(base + t)].astype(f32)
            other = x if residual is None else row_of(residual, i * group + t, rows)
            if k is not None:
                column = (base + t) * LANES + lanes_iota(1)
                mine = (column >= limits[k, 0]) & (column < limits[k + 1, 0])
                x = jnp.where(jnp.broadcast_to(mine, x.shape), x, 0.0)
            return x * other

        @pl.when(first == last)
        def _():
            total = jnp.zeros((rows, LANES), f32)
            for t in range(group):
                total = total + one(t)
            sums[first] += total

        @pl.when(first != last)
        def _():
            def mixed(g, carry):
                def each(k, carry):
                    total = jnp.zeros((rows, LANES), f32)
                    for t in range(BLOCK):
                        total = total + one(g * BLOCK + t, k)
                    sums[k] += total
                    return carry

                begin = ancestry_at(starts, (base + g * BLOCK) * LANES)
                end = ancestry_at(starts, (base + (g + 1) * BLOCK) * LANES - 1)
                lax.fori_loop(begin, end + 1, each, 0)
                return carry

            lax.fori_loop(0, group // BLOCK, mixed, 0)

        return carry

    lax.fori_loop(0, residual.shape[0] // group if residual is not None else tiles // group, body, 0)


def norms_kernel(step, rows_ref, limits, out, sums):
    sums[...] = jnp.zeros_like(sums)
    tiles = rows_ref.shape[1] // LANES
    segment_sums(step, rows_ref, limits, sums, tiles, lambda local: local)
    out[...] = pack_sums(sums)


def scores_kernel(step, count, scale, shift, first, last, rows_ref, limits, *refs):
    parts, rest = refs[:count], refs[count:]
    residual = rest[-1] if not last else rest[-2]
    sums = rest[-2] if not last else rest[-1]
    sums[...] = jnp.zeros_like(sums) if first else rest[0][...]
    per_part = parts[0].shape[0]
    for p, part in enumerate(parts):
        residual[pl.ds(p * per_part, per_part), :] = part[...]
    me = lax.axis_index("var")
    base_of = lambda local: (me ^ (scale * (local // per_part) + shift)) * per_part + local % per_part
    segment_sums(step, rows_ref, limits, sums, per_part, base_of, residual)
    if last:
        norms, out = rest[1:3]
        out[pl.ds(0, SUB), :] = pack_sums(sums)
        out[pl.ds(SUB, SUB), :] = norms[...]


def call(kernel, outs, inputs, scratch=(), limit=8, specs=None):
    return pl.pallas_call(
        kernel,
        out_shape=outs,
        in_specs=specs or [in_vmem] * len(inputs),
        out_specs=jax.tree.map(lambda out: in_vmem, outs),
        scratch_shapes=list(scratch),
        compiler_params=pltpu.CompilerParams(vmem_limit_bytes=limit << 20),
    )(*inputs)


def exchange(array, axis, offset):
    size = lax.axis_size(axis)
    return lax.ppermute(array, axis, [(i, i ^ offset) for i in range(size)])


def gather_ind(array):
    parts, offset = [array], 1
    while offset < lax.axis_size("ind"):
        parts = parts + [exchange(part, "ind", offset) for part in parts]
        offset *= 2
    return parts


def update(
    genotypes, residual, ancestry, effects, prior_precision, noise_var, block_index, gaussians
):
    ancestries, variants = effects.shape
    steps, block = block_index.shape
    people = residual.shape[0]
    var_size = lax.axis_size("var")
    chips = var_size // 2
    tiles = people // LANES
    part = tiles // var_size
    per_chunk = 64
    while tiles % per_chunk:
        per_chunk //= 2
    shape = jax.ShapeDtypeStruct
    in_place = lambda array: pltpu.with_memory_space_constraint(array, pltpu.HBM)
    residual = residual.reshape(tiles, LANES)
    ancestry = ancestry.reshape(tiles, LANES)
    noise_var = noise_var.reshape(1, ancestries)
    gaussians = gaussians.transpose(1, 0, 2)
    inputs = [genotypes, residual, ancestry, block_index, prior_precision, noise_var]

    held, payload, limits, selected, consts, current = call(
        load_kernel,
        (
            pltpu.VMEM((steps * block, people), bf16),
            shape((2 * SUB, LANES), f32),
            shape((SUB, LANES), i32),
            shape((steps * block, variants), f32),
            shape((ancestries * (ancestries + 1), LANES), f32),
            shape((part, LANES), f32),
        ),
        [in_place(array) for array in inputs],
        [
            pltpu.VMEM(genotypes.shape, bf16),
            pltpu.VMEM(residual.shape, f32),
            pltpu.VMEM(ancestry.shape, i32),
            pltpu.SMEM(block_index.shape, i32),
            pltpu.SMEM(prior_precision.shape, f32),
            pltpu.SMEM(noise_var.shape, f32),
            pltpu.VMEM((ancestries, block, LANES), f32),
            pltpu.VMEM((ancestries, block, LANES), f32),
            pltpu.SemaphoreType.DMA((tiles // per_chunk,)),
            pltpu.SemaphoreType.DMA((5,)),
        ],
        32,
        [in_hbm] * len(inputs),
    )
    held = pltpu.with_memory_space_constraint(held, pltpu.VMEM)

    columns_shape = shape((2 * ancestries, block, LANES), f32)
    column_shape = shape((ancestries, block, LANES), f32)
    part_shape = shape((chips, part, LANES), f32)
    effects_shape = shape(effects.shape, f32)
    factor = pltpu.VMEM((ancestries * (ancestries + 1), block, LANES), f32)
    sums_scratch = pltpu.VMEM(column_shape.shape, f32)
    residual_scratch = pltpu.VMEM(((chips - 1) * part, LANES), f32)
    fresh = None
    for s in range(steps):
        if s == 0:
            columns = call(functools.partial(prepare_kernel, s), columns_shape, [selected, effects, gaussians])
        else:
            columns, effects = call(
                functools.partial(prepare_kernel, s),
                (columns_shape, effects_shape),
                [selected, effects, gaussians, fresh],
            )
        parts = gather_ind(payload)
        send, fresh, change = call(
            functools.partial(draw_kernel, s, len(parts)),
            (part_shape, column_shape, column_shape),
            [held, limits, columns, consts, *parts],
            [factor],
        )
        received = exchange(send, "var", 1)
        keep = call(functools.partial(keep_kernel, s), part_shape, [held, limits, change])
        sums = call(pair_kernel, (shape((part, LANES), f32),) * chips, [keep, received])
        arrived = [sums[0]] + [exchange(sums[e], "var", 2 * e) for e in range(1, chips)]
        norms = []
        if s + 1 < steps:
            kernel = functools.partial(norms_kernel, s + 1)
            norms = [call(kernel, shape((SUB, LANES), f32), [held, limits], [sums_scratch])]
        kernel = functools.partial(chip_kernel, chips)
        current = call(kernel, shape((part, LANES), f32), [current, *arrived, *norms])
        if s + 1 == steps:
            effects = call(functools.partial(commit_kernel, s), effects_shape, [selected, effects, fresh])
            break
        even = [current] + [exchange(current, "var", 2 * e) for e in range(1, chips)]
        odd = [exchange(one, "var", 1) for one in even]
        scores = functools.partial(scores_kernel, s + 1)
        partial = call(
            functools.partial(scores, 2, 1, 0, True, False),
            column_shape,
            [held, limits, even[0], odd[0]],
            [pltpu.VMEM((2 * part, LANES), f32)],
        )
        partial = call(
            functools.partial(scores, chips - 1, 2, 2, False, False),
            column_shape,
            [held, limits, *even[1:], partial],
            [residual_scratch],
        )
        payload = call(
            functools.partial(scores, chips - 1, 2, 3, False, True),
            shape((2 * SUB, LANES), f32),
            [held, limits, *odd[1:], partial, *norms],
            [residual_scratch, sums_scratch],
        )
    return current.reshape(-1), effects


def solution(mesh):
    return jax.shard_map(
        update,
        mesh=mesh,
        in_specs=(
            P("var", "ind"),
            P("ind"),
            P("ind"),
            P(None, "var"),
            P(),
            P(),
            P(None, "var"),
            P(None, None, "var"),
        ),
        out_specs=(P(("ind", "var")), P(None, "var")),
        check_vma=False,
    )
```
